32 devices in a mesh: dp: 8 (over y, x, core), tensor: 4 (over z).
Axes of the slice: x: 2, y: 2, z: 4, core: 2. Of those that a mesh axis runs over, the one named last changes fastest.
Arguments:
- inputs: bfloat16 [2, 1024, 1024], P(None, ('dp', 'tensor')), may hold values from -6 to 6
- out_grad: bfloat16 [2, 1024, 1024], P(None, ('dp', 'tensor')), may hold values from -6 to 6
- saved: bfloat16 [2, 1024, 32768], P(None, 'dp', 'tensor'), may hold values from 0 to 16, as said below
- w_in: bfloat16 [1024, 32768], P(None, 'tensor'), may hold values from -0.1875 to 0.1875
- w_out: bfloat16 [1024, 32768], P(None, 'tensor'), may hold values from -0.03125 to 0.03125
- mom_in: float32 [1024, 32768], P('dp', 'tensor'), may hold values from -3 to 3
Outputs:
- in_grad: float32 [2, 1024, 1024], P(None, ('dp', 'tensor'))
- new_mom_in: float32 [1024, 32768], P('dp', 'tensor')
The draws below stay inside these ranges and needn't reach their ends.
Inputs may be any that keep to these rules, and one draw needn't show every extreme that they name: `saved`: every entry is zero or positive.
All inputs are finite; a program needn't handle non-finite values.
Results may differ from the reference program's by a relative error of at most 0.0029.
Values may be sent and summed in bfloat16 or wider, within the bound.
A program may use at most 128 MiB of HBM per device.

```python
import jax
import jax.numpy as jnp
from jax import lax

D = 1024
FF = 32768
MICRO = 2
ROWS = 128
TOKENS = 1024
N_DP = 8


def draw_saved(key, part):
    shape = (MICRO, TOKENS, FF)
    values = jax.random.normal(key, shape, jnp.float32)
    return jnp.maximum(values, 0.0).astype(jnp.bfloat16)


def spiked(entries, own_key, source, target, parts, factor):
    def block_of(position):
        return (jnp.arange(entries.shape[position]) // (entries.shape[position] // parts)).reshape((-1,) + (1,) * (entries.ndim - 1 - position))

    one_side = jax.random.permutation(own_key, parts)[block_of(target)]
    far = (block_of(target) + parts // 2) % parts
    return jnp.where((block_of(source) == one_side) | (block_of(source) == far), factor * entries, entries)


def shard_levels(rng, dims, cuts, smallest, top_value):
    def one(position, parts):
        heights = jax.random.uniform(jax.random.fold_in(jax.random.fold_in(rng, 6), position), (parts,), jnp.float32, smallest / len(cuts), top_value / len(cuts))
        return jnp.repeat(jnp.exp(heights), dims[position] // parts).reshape((-1,) + (1,) * (len(dims) - position - 1))

    gain = one(*cuts[0])
    for cut in cuts[1:]:
        gain = gain * one(*cut)
    return gain


def normal_values(stream_key, dims, scale, reach, split=(), held_as=jnp.bfloat16):
    loudness = shard_levels(stream_key, dims, split, -0.22, 0.18) if split else 1.0
    result = jax.random.normal(stream_key, dims, jnp.float32) * scale * loudness
    return jnp.minimum(jnp.maximum(result, -reach), reach).astype(held_as)


def noise_with(own_key, shape, width, most, pieces, heavy, held_as=jnp.bfloat16):
    entries = width * jax.random.normal(own_key, shape, jnp.float32)
    if pieces:
        entries = entries * shard_levels(own_key, shape, pieces, -0.22, 0.18)
    return jnp.clip(spiked(entries, jax.random.fold_in(own_key, 3), *heavy), -most, most).astype(held_as)


def setup_inputs(seed: int = 0) -> dict:
    streams_of = jax.random.split(jax.random.key(seed), 7)
    return {
        "inputs": noise_with(streams_of[0], (MICRO, TOKENS, D), 1.0, 6.0, ((1, 32),), (1, 2, 32, 2.75)),
        "out_grad": noise_with(streams_of[1], (MICRO, TOKENS, D), 1.0, 6.0, ((1, 32),), (1, 2, 32, 2.75)),
        "saved": draw_saved(jax.random.fold_in(streams_of[6], 71), 0),
        "w_in": normal_values(streams_of[3], (D, FF), D ** -0.5, 0.1875, ((1, 4),)),
        "w_out": normal_values(streams_of[4], (D, FF), FF ** -0.5, 0.03125, ((1, 4),)),
        "mom_in": normal_values(streams_of[5], (D, FF), 0.5, 3.0, ((0, 8), (1, 4)), jnp.float32),
    }


momentum_decay = 0.9


def regroup(values):
    micro_count, token_count, last_width = values.shape
    group_count = token_count // ROWS
    shaped = values.reshape(micro_count, group_count, ROWS, last_width).transpose(1, 0, 2, 3)
    return shaped.reshape(group_count, micro_count * ROWS, last_width)


def reference(inputs, out_grad, saved, w_in, w_out, mom_in):
    def group_step(total_in, entry):
        token_rows, grad_rows, saved_rows = entry
        product = jnp.dot(grad_rows, w_out, preferred_element_type=jnp.float32)
        hidden_rows = jnp.where(saved_rows > 0, product, jnp.zeros_like(product)).astype(jnp.bfloat16)
        input_rows = jnp.dot(hidden_rows, w_in.T, preferred_element_type=jnp.float32)
        part_in = jnp.dot(token_rows.T, hidden_rows, preferred_element_type=jnp.float32)
        return total_in + part_in, input_rows

    zero_grads = jnp.zeros(w_in.shape, jnp.float32)
    total_in, input_rows = lax.scan(
        group_step, zero_grads, (regroup(inputs), regroup(out_grad), regroup(saved)))
    in_grad = input_rows.reshape(N_DP, MICRO, ROWS, D).transpose(1, 0, 2, 3).reshape(MICRO, N_DP * ROWS, D)
    new_mom_in = momentum_decay * mom_in + total_in / N_DP
    return in_grad, new_mom_in
```

```python
import jax
import jax.numpy as jnp
from jax import lax
from jax.sharding import PartitionSpec as P

momentum_decay = 0.9
PIECES = 2
SMALL_AXIS = 8


def xor_send(value, size, mask):
    return lax.ppermute(value, "dp", [(i, i ^ mask) for i in range(size)])


def gather_rows(value):
    size = lax.axis_size("tensor")
    if size > SMALL_AXIS:
        return lax.all_gather(value, "tensor", axis=1, tiled=True)
    me = lax.axis_index("tensor")
    rows = value.shape[1]
    shape = (value.shape[0], rows * size) + value.shape[2:]
    moved = [value] + [
        lax.ppermute(value, "tensor", [(i, (i + k) % size) for i in range(size)])
        for k in range(1, size)
    ]
    full = jnp.zeros(shape, value.dtype)
    for k, piece in enumerate(moved):
        start = (me - k + size) % size * rows
        full = lax.dynamic_update_slice_in_dim(full, piece, start, axis=1)
    return full


def scatter_rows(terms):
    size = lax.axis_size("tensor")
    if size > SMALL_AXIS:
        return lax.psum_scatter(terms, "tensor", scatter_dimension=1, tiled=True)
    me = lax.axis_index("tensor")
    rows = terms.shape[1] // size
    total = lax.dynamic_slice_in_dim(terms, me * rows, rows, axis=1)
    for k in range(1, size):
        start = (me + k) % size * rows
        piece = lax.dynamic_slice_in_dim(terms, start, rows, axis=1).astype(jnp.bfloat16)
        got = lax.ppermute(piece, "tensor", [(i, (i + k) % size) for i in range(size)])
        total = total + got.astype(jnp.float32)
    return total


def spans(bits):
    masks = [0]
    for bit in bits:
        masks = masks + [m | bit for m in masks]
    return masks


def transpose_dot(left_rows, right_rows):
    return lax.dot_general(
        left_rows, right_rows, (((0,), (0,)), ((), ())), preferred_element_type=jnp.float32
    )


def body(inputs, out_grad, saved, w_in, w_out, mom_in):
    micro_count, shard_rows, model_width = inputs.shape
    hidden_width = saved.shape[2]
    size = lax.axis_size("dp")
    me = lax.axis_index("dp")
    own_rows = model_width // size
    bits = [1 << b for b in range(1, size.bit_length() - 1)]
    orders = [(bits[0], bits[1:]), (bits[-1], bits[:-1])]

    def columns_of(owner, masks):
        return jnp.concatenate(
            [
                lax.dynamic_slice_in_dim(inputs, (owner ^ m) * own_rows, own_rows, axis=2)
                for m in masks
            ],
            axis=2,
        )

    grad_rows = gather_rows(out_grad).reshape(-1, model_width)

    pieces = []
    for first, rest in orders:
        masks = spans(rest)
        pieces.append(columns_of(me, masks))
        for m in (1, first, first | 1):
            pieces.append(xor_send(columns_of(me ^ m, masks), size, m))
    packed = jnp.concatenate(pieces, axis=2)
    packed, grad_rows = lax.optimization_barrier((packed, grad_rows))
    packed = gather_rows(packed)
    packed = packed.reshape(-1, packed.shape[2])
    width = packed.shape[1] // (4 * len(orders))

    saved_rows = saved.reshape(-1, hidden_width)
    half = hidden_width // len(orders)
    step = half // PIECES

    hidden_parts = {}
    for p in range(PIECES):
        for o in range(len(orders)):
            start = o * half + p * step
            product = jnp.dot(
                grad_rows, w_out[:, start:start + step], preferred_element_type=jnp.float32
            )
            mask = saved_rows[:, start:start + step] > 0
            hidden_parts[start] = jnp.where(mask, product, 0.0).astype(jnp.bfloat16)

    results = {}
    for p in range(PIECES):
        for o, (first, rest) in enumerate(orders):
            start = o * half + p * step
            own = hidden_parts[start]
            near = xor_send(own, size, first)
            pair = xor_send(own, size, 1)
            near_pair = xor_send(near, size, 1)
            tokens = packed[:, o * 4 * width:(o + 1) * 4 * width]
            terms = [tokens[:, i * width:(i + 1) * width] for i in range(4)]
            total = transpose_dot(terms[0], own) + transpose_dot(terms[1], pair)
            total = total + transpose_dot(terms[2], near) + transpose_dot(terms[3], near_pair)
            kept = total[:own_rows]
            for i, m in enumerate(spans(rest)):
                if m:
                    part = total[i * own_rows:(i + 1) * own_rows].astype(jnp.bfloat16)
                    kept = kept + xor_send(part, size, m).astype(jnp.float32)
            old = mom_in[:, start:start + step]
            results[start] = momentum_decay * old + kept / size
    new_mom_in = jnp.concatenate([results[s] for s in sorted(results)], axis=1)

    hidden = jnp.concatenate([hidden_parts[s] for s in sorted(hidden_parts)], axis=1)
    input_terms = lax.dot_general(
        hidden, w_in, (((1,), (1,)), ((), ())), preferred_element_type=jnp.float32
    ).reshape(micro_count, -1, model_width)
    in_grad = scatter_rows(input_terms)
    return (in_grad, new_mom_in)


def solution(mesh):
    placed = (
        P(None, ("dp", "tensor"), None),
        P(None, ("dp", "tensor"), None),
        P(None, "dp", "tensor"),
        P(None, "tensor"),
        P(None, "tensor"),
        P("dp", "tensor"),
    )
    return jax.shard_map(
        body,
        mesh=mesh,
        in_specs=placed,
        out_specs=(P(None, ("dp", "tensor"), None), P("dp", "tensor")),
        check_vma=False,
    )
```

```python
import jax
import jax.numpy as jnp
from jax import lax
from jax.sharding import PartitionSpec as P


momentum_decay = 0.9
PIECES = 2
SMALL_AXIS = 8


def xor_send(value, size, mask):
    return lax.ppermute(value, "dp", [(i, i ^ mask) for i in range(size)])


def gather_rows(value):
    size = lax.axis_size("tensor")
    if size > SMALL_AXIS:
        return lax.all_gather(value, "tensor", axis=1, tiled=True)
    me = lax.axis_index("tensor")
    rows = value.shape[1]
    shape = (value.shape[0], rows * size) + value.shape[2:]
    moved = [value] + [
        lax.ppermute(value, "tensor", [(i, (i + k) % size) for i in range(size)])
        for k in range(1, size)
    ]
    full = jnp.zeros(shape, value.dtype)
    for k, piece in enumerate(moved):
        start = (me - k + size) % size * rows
        full = lax.dynamic_update_slice_in_dim(full, piece, start, axis=1)
    return full


def scatter_rows(terms):
    size = lax.axis_size("tensor")
    if size > SMALL_AXIS:
        return lax.psum_scatter(terms, "tensor", scatter_dimension=1, tiled=True)
    me = lax.axis_index("tensor")
    rows = terms.shape[1] // size
    total = lax.dynamic_slice_in_dim(terms, me * rows, rows, axis=1)
    for k in range(1, size):
        start = (me + k) % size * rows
        piece = lax.dynamic_slice_in_dim(terms, start, rows, axis=1).astype(jnp.bfloat16)
        got = lax.ppermute(piece, "tensor", [(i, (i + k) % size) for i in range(size)])
        total = total + got.astype(jnp.float32)
    return total


def spans(bits):
    masks = [0]
    for bit in bits:
        masks = masks + [m | bit for m in masks]
    return masks


def transpose_dot(left_rows, right_rows):
    return lax.dot_general(
        left_rows, right_rows, (((0,), (0,)), ((), ())), preferred_element_type=jnp.float32
    )


def step_body(inputs, out_grad, saved, w_in, w_out, mom_in):
    micro_count, _, model_width = inputs.shape
    hidden_width = saved.shape[2]
    size = lax.axis_size("dp")
    me = lax.axis_index("dp")
    own_rows = model_width // size
    bits = [1 << b for b in range(1, size.bit_length() - 1)]
    orders = [(bits[0], bits[1:]), (bits[-1], bits[:-1])]

    def columns_of(owner, masks):
        return jnp.concatenate(
            [
                lax.dynamic_slice_in_dim(inputs, (owner ^ m) * own_rows, own_rows, axis=2)
                for m in masks
            ],
            axis=2,
        )

    grad_rows = gather_rows(out_grad).reshape(-1, model_width)

    pieces = []
    for first, rest in orders:
        masks = spans(rest)
        pieces.append(columns_of(me, masks))
        for m in (1, first, first | 1):
            pieces.append(xor_send(columns_of(me ^ m, masks), size, m))
    packed = jnp.concatenate(pieces, axis=2)
    packed, grad_rows = lax.optimization_barrier((packed, grad_rows))
    packed = gather_rows(packed)
    packed = packed.reshape(-1, packed.shape[2])
    width = packed.shape[1] // (4 * len(orders))

    saved_rows = saved.reshape(-1, hidden_width)
    half = hidden_width // len(orders)
    step = half // PIECES
    chunks = [(o, o * half + p * step) for p in range(PIECES) for o in range(len(orders))]

    hidden, near, pair = [], [], []
    for c, (o, start) in enumerate(chunks):
        product = jnp.dot(
            grad_rows, w_out[:, start:start + step], preferred_element_type=jnp.float32
        )
        mask = saved_rows[:, start:start + step] > 0
        hidden.append(jnp.where(mask, product, 0.0).astype(jnp.bfloat16))
        near.append(xor_send(hidden[c], size, orders[o][0]))
        pair.append(xor_send(hidden[c], size, 1))

    ordered = [hidden[c] for c in sorted(range(len(chunks)), key=lambda c: chunks[c][1])]
    input_terms = lax.dot_general(
        jnp.concatenate(ordered, axis=1), w_in, (((1,), (1,)), ((), ())),
        preferred_element_type=jnp.float32,
    ).reshape(micro_count, -1, model_width)
    in_grad = scatter_rows(input_terms)

    new_mom_in = momentum_decay * mom_in
    arrived = []
    for c, (o, start) in enumerate(chunks):
        first, rest = orders[o]
        tokens = packed[:, o * 4 * width:(o + 1) * 4 * width]
        terms = [tokens[:, i * width:(i + 1) * width] for i in range(4)]
        early = transpose_dot(terms[0], hidden[c]) + transpose_dot(terms[1], pair[c])
        early = lax.optimization_barrier(early)
        near_pair = xor_send(near[c], size, 1)
        total = early + transpose_dot(terms[2], near[c])
        total = total + transpose_dot(terms[3], near_pair)
        kept = total[:own_rows]
        for i, m in enumerate(spans(rest)):
            if m:
                part = total[i * own_rows:(i + 1) * own_rows].astype(jnp.bfloat16)
                arrived.append((c, xor_send(part, size, m)))
        old = new_mom_in[:, start:start + step]
        new_mom_in = new_mom_in.at[:, start:start + step].set(old + kept / size)
    for c, part in arrived:
        start = chunks[c][1]
        old = new_mom_in[:, start:start + step]
        update = old + part.astype(jnp.float32) / size
        new_mom_in = new_mom_in.at[:, start:start + step].set(update)
    return (in_grad, new_mom_in)


def solution(mesh):
    placed = (
        P(None, ("dp", "tensor"), None),
        P(None, ("dp", "tensor"), None),
        P(None, "dp", "tensor"),
        P(None, "tensor"),
        P(None, "tensor"),
        P("dp", "tensor"),
    )
    return jax.shard_map(
        step_body,
        mesh=mesh,
        in_specs=placed,
        out_specs=(P(None, ("dp", "tensor"), None), P("dp", "tensor")),
        check_vma=False,
    )
```

```python
import jax
import jax.numpy as jnp
from jax import lax
from jax.experimental import pallas as pl
from jax.experimental.pallas import tpu as pltpu
from jax.sharding import PartitionSpec as P


momentum_decay = 0.9
PIECES = 2
SMALL_AXIS = 8
TILE = 512
KERNEL_BYTES = 16 << 20


def xor_send(value, size, mask):
    return lax.ppermute(value, "dp", [(i, i ^ mask) for i in range(size)])


def gather_rows(value):
    size = lax.axis_size("tensor")
    if size > SMALL_AXIS:
        return lax.all_gather(value, "tensor", axis=1, tiled=True)
    me = lax.axis_index("tensor")
    rows = value.shape[1]
    shape = (value.shape[0], rows * size) + value.shape[2:]
    moved = [value] + [
        lax.ppermute(value, "tensor", [(i, (i + k) % size) for i in range(size)])
        for k in range(1, size)
    ]
    full = jnp.zeros(shape, value.dtype)
    for k, piece in enumerate(moved):
        start = (me - k + size) % size * rows
        full = lax.dynamic_update_slice_in_dim(full, piece, start, axis=1)
    return full


def scatter_rows(terms):
    size = lax.axis_size("tensor")
    if size > SMALL_AXIS:
        return lax.psum_scatter(terms, "tensor", scatter_dimension=1, tiled=True)
    me = lax.axis_index("tensor")
    rows = terms.shape[1] // size
    total = lax.dynamic_slice_in_dim(terms, me * rows, rows, axis=1)
    for k in range(1, size):
        start = (me + k) % size * rows
        piece = lax.dynamic_slice_in_dim(terms, start, rows, axis=1).astype(jnp.bfloat16)
        got = lax.ppermute(piece, "tensor", [(i, (i + k) % size) for i in range(size)])
        total = total + got.astype(jnp.float32)
    return total


def spans(bits):
    masks = [0]
    for bit in bits:
        masks = masks + [m | bit for m in masks]
    return masks


def hidden_kernel(grad_ref, saved_ref, w_ref, out_ref):
    product = jnp.dot(grad_ref[...], w_ref[...], preferred_element_type=jnp.float32)
    out_ref[...] = jnp.where(saved_ref[...] > 0, product, 0.0).astype(jnp.bfloat16)


def hidden_chunk(grad_rows, saved_rows, w_out, start, step):
    rows, depth = grad_rows.shape
    tile = min(TILE, step)
    first = start // tile
    return pl.pallas_call(
        hidden_kernel,
        grid=(step // tile,),
        out_shape=jax.ShapeDtypeStruct((rows, step), jnp.bfloat16),
        in_specs=[
            pl.BlockSpec((rows, depth), lambda j: (0, 0)),
            pl.BlockSpec((rows, tile), lambda j: (0, first + j)),
            pl.BlockSpec((depth, tile), lambda j: (0, first + j)),
        ],
        out_specs=pl.BlockSpec((rows, tile), lambda j: (0, j)),
        cost_estimate=pl.CostEstimate(
            flops=2 * rows * depth * step, bytes_accessed=2 * step * (depth + 2 * rows),
            transcendentals=0,
        ),
        compiler_params=pltpu.CompilerParams(vmem_limit_bytes=KERNEL_BYTES),
    )(grad_rows, saved_rows, w_out)


def gradient_kernel(size, tokens_ref, own_ref, pair_ref, near_ref, far_ref, mom_ref, base_ref, part_ref):
    width = tokens_ref.shape[0] // 4
    total = None
    for i, ref in enumerate((own_ref, pair_ref, near_ref, far_ref)):
        term = jnp.dot(
            tokens_ref[i * width:(i + 1) * width, :], ref[...],
            preferred_element_type=jnp.float32,
        )
        total = term if total is None else total + term
    kept = base_ref.shape[0]
    base_ref[...] = momentum_decay * mom_ref[...] + total[:kept] / size
    part_ref[...] = total[kept:].astype(jnp.bfloat16)


def gradient_chunk(size, tokens, which, rows_of, mom_in, start):
    rows, step = rows_of[0].shape
    kept = mom_in.shape[0]
    total = tokens.shape[0] // 2
    width = total // 4
    tile = min(TILE, step)
    first = start // tile
    block = pl.BlockSpec((rows, tile), lambda j: (0, j))
    return pl.pallas_call(
        lambda *refs: gradient_kernel(size, *refs),
        grid=(step // tile,),
        out_shape=(
            jax.ShapeDtypeStruct((kept, step), jnp.float32),
            jax.ShapeDtypeStruct((width - kept, step), jnp.bfloat16),
        ),
        in_specs=[
            pl.BlockSpec((total, rows), lambda j: (which, 0)),
            block, block, block, block,
            pl.BlockSpec((kept, tile), lambda j: (0, first + j)),
        ],
        out_specs=(
            pl.BlockSpec((kept, tile), lambda j: (0, j)),
            pl.BlockSpec((width - kept, tile), lambda j: (0, j)),
        ),
        cost_estimate=pl.CostEstimate(
            flops=2 * rows * total * step, bytes_accessed=8 * rows * step, transcendentals=0
        ),
        compiler_params=pltpu.CompilerParams(vmem_limit_bytes=KERNEL_BYTES),
    )(tokens, *rows_of, mom_in)


def finish_kernel(size, count, base_ref, *refs):
    total = refs[0][...].astype(jnp.float32)
    for ref in refs[1:count]:
        total = total + ref[...].astype(jnp.float32)
    refs[-1][...] = base_ref[...] + total / size


def finish_chunk(size, base, parts, start, whole_width, result):
    kept, step = base.shape
    tile = min(2 * TILE, step)
    first = start // tile
    block = pl.BlockSpec((kept, tile), lambda j: (0, j))
    operands = [base, *parts]
    specs = [block] * len(operands)
    aliases = {}
    if result is not None:
        aliases = {len(operands): 0}
        operands.append(result)
        specs.append(pl.BlockSpec(memory_space=pl.ANY))
    return pl.pallas_call(
        lambda *refs: finish_kernel(size, len(parts), *refs),
        grid=(step // tile,),
        out_shape=jax.ShapeDtypeStruct((kept, whole_width), jnp.float32),
        in_specs=specs,
        out_specs=pl.BlockSpec((kept, tile), lambda j: (0, first + j)),
        input_output_aliases=aliases,
        cost_estimate=pl.CostEstimate(
            flops=2 * kept * step, bytes_accessed=10 * kept * step, transcendentals=0
        ),
        compiler_params=pltpu.CompilerParams(vmem_limit_bytes=KERNEL_BYTES),
    )(*operands)


def step_body(inputs, out_grad, saved, w_in, w_out, mom_in):
    micro_count, _, model_width = inputs.shape
    hidden_width = saved.shape[2]
    size = lax.axis_size("dp")
    me = lax.axis_index("dp")
    own_rows = model_width // size
    bits = [1 << b for b in range(1, size.bit_length() - 1)]
    orders = [(bits[0], bits[1:]), (bits[-1], bits[:-1])]

    def columns_of(owner, masks):
        return jnp.concatenate(
            [
                lax.dynamic_slice_in_dim(inputs, (owner ^ m) * own_rows, own_rows, axis=2)
                for m in masks
            ],
            axis=2,
        )

    grad_rows = gather_rows(out_grad).reshape(-1, model_width)

    pieces = []
    for first, rest in orders:
        masks = spans(rest)
        pieces.append(columns_of(me, masks))
        for m in (1, first, first | 1):
            pieces.append(xor_send(columns_of(me ^ m, masks), size, m))
    packed = jnp.concatenate(pieces, axis=2)
    packed, grad_rows = lax.optimization_barrier((packed, grad_rows))
    packed = gather_rows(packed)
    tokens = packed.reshape(-1, packed.shape[2]).T

    saved_rows = saved.reshape(-1, hidden_width)
    half = hidden_width // len(orders)
    step = half // PIECES
    chunks = [(o, o * half + p * step) for p in range(PIECES) for o in range(len(orders))]

    hidden, near, pair = [], [], []
    for c, (o, start) in enumerate(chunks):
        hidden.append(hidden_chunk(grad_rows, saved_rows, w_out, start, step))
        near.append(xor_send(hidden[c], size, orders[o][0]))
        pair.append(xor_send(hidden[c], size, 1))

    ordered = [hidden[c] for c in sorted(range(len(chunks)), key=lambda c: chunks[c][1])]
    input_terms = lax.dot_general(
        jnp.concatenate(ordered, axis=1), w_in, (((1,), (1,)), ((), ())),
        preferred_element_type=jnp.float32,
    ).reshape(micro_count, -1, model_width)
    in_grad = scatter_rows(input_terms)

    waiting = []
    for c, (o, start) in enumerate(chunks):
        first, rest = orders[o]
        near_pair = xor_send(near[c], size, 1)
        base, part = gradient_chunk(
            size, tokens, o, (hidden[c], pair[c], near[c], near_pair), mom_in, start
        )
        parts = [
            xor_send(part[(i - 1) * own_rows:i * own_rows], size, m)
            for i, m in enumerate(spans(rest))
            if m
        ]
        waiting.append((start, base, parts))
    new_mom_in = None
    for start, base, parts in waiting:
        new_mom_in = finish_chunk(size, base, parts, start, hidden_width, new_mom_in)
    return (in_grad, new_mom_in)


def solution(mesh):
    placed = (
        P(None, ("dp", "tensor"), None),
        P(None, ("dp", "tensor"), None),
        P(None, "dp", "tensor"),
        P(None, "tensor"),
        P(None, "tensor"),
        P("dp", "tensor"),
    )
    return jax.shard_map(
        step_body,
        mesh=mesh,
        in_specs=placed,
        out_specs=(P(None, ("dp", "tensor"), None), P("dp", "tensor")),
        check_vma=False,
    )
```

```python
import jax
import jax.numpy as jnp
from jax import lax
from jax.experimental import pallas as pl
from jax.sharding import PartitionSpec as P


momentum_decay = 0.9
PIECES = 2
SMALL_AXIS = 8
TILE = 512


def xor_send(value, size, mask):
    return lax.ppermute(value, "dp", [(i, i ^ mask) for i in range(size)])


def gather_rows(value):
    size = lax.axis_size("tensor")
    if size > SMALL_AXIS:
        return lax.all_gather(value, "tensor", axis=1, tiled=True)
    me = lax.axis_index("tensor")
    rows = value.shape[1]
    shape = (value.shape[0], rows * size) + value.shape[2:]
    moved = [value] + [
        lax.ppermute(value, "tensor", [(i, (i + k) % size) for i in range(size)])
        for k in range(1, size)
    ]
    full = jnp.zeros(shape, value.dtype)
    for k, piece in enumerate(moved):
        start = (me - k + size) % size * rows
        full = lax.dynamic_update_slice_in_dim(full, piece, start, axis=1)
    return full


def scatter_rows(terms):
    size = lax.axis_size("tensor")
    if size > SMALL_AXIS:
        return lax.psum_scatter(terms, "tensor", scatter_dimension=1, tiled=True)
    me = lax.axis_index("tensor")
    rows = terms.shape[1] // size
    total = lax.dynamic_slice_in_dim(terms, me * rows, rows, axis=1)
    for k in range(1, size):
        start = (me + k) % size * rows
        piece = lax.dynamic_slice_in_dim(terms, start, rows, axis=1).astype(jnp.bfloat16)
        got = lax.ppermute(piece, "tensor", [(i, (i + k) % size) for i in range(size)])
        total = total + got.astype(jnp.float32)
    return total


def spans(bits):
    masks = [0]
    for bit in bits:
        masks = masks + [m | bit for m in masks]
    return masks


def hidden_kernel(grad_ref, saved_ref, w_ref, out_ref):
    product = jnp.dot(grad_ref[...], w_ref[...], preferred_element_type=jnp.float32)
    out_ref[...] = jnp.where(saved_ref[...] > 0, product, 0.0).astype(jnp.bfloat16)


def hidden_chunk(grad_rows, saved_rows, w_out, start, step):
    rows, depth = grad_rows.shape
    tile = min(TILE, step)
    first = start // tile
    return pl.pallas_call(
        hidden_kernel,
        grid=(step // tile,),
        out_shape=jax.ShapeDtypeStruct((rows, step), jnp.bfloat16),
        in_specs=[
            pl.BlockSpec((rows, depth), lambda j: (0, 0)),
            pl.BlockSpec((rows, tile), lambda j: (0, first + j)),
            pl.BlockSpec((depth, tile), lambda j: (0, first + j)),
        ],
        out_specs=pl.BlockSpec((rows, tile), lambda j: (0, j)),
        cost_estimate=pl.CostEstimate(
            flops=2 * rows * depth * step, bytes_accessed=2 * step * (depth + 2 * rows),
            transcendentals=0,
        ),
    )(grad_rows, saved_rows, w_out)


def gradient_kernel(size, tokens_ref, own_ref, pair_ref, near_ref, far_ref, mom_ref, base_ref, part_ref):
    width = tokens_ref.shape[1] // 4
    total = None
    for i, ref in enumerate((own_ref, pair_ref, near_ref, far_ref)):
        term = lax.dot_general(
            tokens_ref[:, i * width:(i + 1) * width], ref[...], (((0,), (0,)), ((), ())),
            preferred_element_type=jnp.float32,
        )
        total = term if total is None else total + term
    kept = base_ref.shape[0]
    base_ref[...] = momentum_decay * mom_ref[...] + total[:kept] / size
    part_ref[...] = total[kept:].astype(jnp.bfloat16)


def gradient_chunk(size, tokens, which, rows_of, mom_in, start):
    rows, step = rows_of[0].shape
    kept = mom_in.shape[0]
    total = tokens.shape[1] // 2
    width = total // 4
    tile = min(TILE, step)
    first = start // tile
    block = pl.BlockSpec((rows, tile), lambda j: (0, j))
    return pl.pallas_call(
        lambda *refs: gradient_kernel(size, *refs),
        grid=(step // tile,),
        out_shape=(
            jax.ShapeDtypeStruct((kept, step), jnp.float32),
            jax.ShapeDtypeStruct((width - kept, step), jnp.bfloat16),
        ),
        in_specs=[
            pl.BlockSpec((rows, total), lambda j: (0, which)),
            block, block, block, block,
            pl.BlockSpec((kept, tile), lambda j: (0, first + j)),
        ],
        out_specs=(
            pl.BlockSpec((kept, tile), lambda j: (0, j)),
            pl.BlockSpec((width - kept, tile), lambda j: (0, j)),
        ),
        cost_estimate=pl.CostEstimate(
            flops=2 * rows * total * step, bytes_accessed=8 * rows * step, transcendentals=0
        ),
    )(tokens, *rows_of, mom_in)


def finish_kernel(size, count, base_ref, *refs):
    total = refs[0][...].astype(jnp.float32)
    for ref in refs[1:count]:
        total = total + ref[...].astype(jnp.float32)
    refs[-1][...] = base_ref[...] + total / size


def finish_chunk(size, base, parts, start, whole_width, result):
    kept, step = base.shape
    tile = min(2 * TILE, step)
    first = start // tile
    block = pl.BlockSpec((kept, tile), lambda j: (0, j))
    operands = [base, *parts]
    specs = [block] * len(operands)
    aliases = {}
    if result is not None:
        aliases = {len(operands): 0}
        operands.append(result)
        specs.append(pl.BlockSpec(memory_space=pl.ANY))
    return pl.pallas_call(
        lambda *refs: finish_kernel(size, len(parts), *refs),
        grid=(step // tile,),
        out_shape=jax.ShapeDtypeStruct((kept, whole_width), jnp.float32),
        in_specs=specs,
        out_specs=pl.BlockSpec((kept, tile), lambda j: (0, first + j)),
        input_output_aliases=aliases,
        cost_estimate=pl.CostEstimate(
            flops=2 * kept * step, bytes_accessed=10 * kept * step, transcendentals=0
        ),
    )(*operands)


def step_body(inputs, out_grad, saved, w_in, w_out, mom_in):
    micro_count, _, model_width = inputs.shape
    hidden_width = saved.shape[2]
    size = lax.axis_size("dp")
    me = lax.axis_index("dp")
    own_rows = model_width // size
    bits = [1 << b for b in range(1, size.bit_length() - 1)]
    orders = [(bits[0], bits[1:]), (bits[-1], bits[:-1])]

    def columns_of(owner, masks):
        return jnp.concatenate(
            [
                lax.dynamic_slice_in_dim(inputs, (owner ^ m) * own_rows, own_rows, axis=2)
                for m in masks
            ],
            axis=2,
        )

    grad_rows = gather_rows(out_grad).reshape(-1, model_width)

    pieces = []
    for first, rest in orders:
        masks = spans(rest)
        pieces.append(columns_of(me, masks))
        for m in (1, first, first | 1):
            pieces.append(xor_send(columns_of(me ^ m, masks), size, m))
    packed = jnp.concatenate(pieces, axis=2)
    packed, grad_rows = lax.optimization_barrier((packed, grad_rows))
    packed = gather_rows(packed)
    tokens = packed.reshape(-1, packed.shape[2])

    saved_rows = saved.reshape(-1, hidden_width)
    half = hidden_width // len(orders)
    step = half // PIECES
    chunks = [(o, o * half + p * step) for p in range(PIECES) for o in range(len(orders))]

    hidden, near, pair = [], [], []
    for c, (o, start) in enumerate(chunks):
        hidden.append(hidden_chunk(grad_rows, saved_rows, w_out, start, step))
        near.append(xor_send(hidden[c], size, orders[o][0]))
        pair.append(xor_send(hidden[c], size, 1))

    ordered = [hidden[c] for c in sorted(range(len(chunks)), key=lambda c: chunks[c][1])]
    input_terms = lax.dot_general(
        jnp.concatenate(ordered, axis=1), w_in, (((1,), (1,)), ((), ())),
        preferred_element_type=jnp.float32,
    ).reshape(micro_count, -1, model_width)
    in_grad = scatter_rows(input_terms)

    waiting = []
    for c, (o, start) in enumerate(chunks):
        first, rest = orders[o]
        near_pair = xor_send(near[c], size, 1)
        base, part = gradient_chunk(
            size, tokens, o, (hidden[c], pair[c], near[c], near_pair), mom_in, start
        )
        parts = [
            xor_send(part[(i - 1) * own_rows:i * own_rows], size, m)
            for i, m in enumerate(spans(rest))
            if m
        ]
        waiting.append((start, base, parts))
    new_mom_in = None
    for start, base, parts in waiting:
        new_mom_in = finish_chunk(size, base, parts, start, hidden_width, new_mom_in)
    return (in_grad, new_mom_in)


def solution(mesh):
    placed = (
        P(None, ("dp", "tensor"), None),
        P(None, ("dp", "tensor"), None),
        P(None, "dp", "tensor"),
        P(None, "tensor"),
        P(None, "tensor"),
        P("dp", "tensor"),
    )
    return jax.shard_map(
        step_body,
        mesh=mesh,
        in_specs=placed,
        out_specs=(P(None, ("dp", "tensor"), None), P("dp", "tensor")),
        check_vma=False,
    )
```
